32 devices in a mesh: dp: 2 (over x), hist: 16 (over z, y, core).
Axes of the slice: x: 2, y: 2, z: 4, core: 2. Of those that a mesh axis runs over, the one named last changes fastest.
Arguments:
- queries: bfloat16 [2, 8192, 512], P('dp', 'hist'), may hold values from -6 to 6
- key_rows: bfloat16 [2, 8192, 512], P('dp', 'hist'), may hold values from -6 to 6
- value_rows: bfloat16 [2, 8192, 512], P('dp', 'hist'), may hold values from -6 to 6
- gate_rows: bfloat16 [2, 8192, 512], P('dp', 'hist'), may hold values from -6 to 6
- user_start: int32 [2, 8192], P('dp', 'hist'), may hold values from 0 to 8191, as said below
- w_out: bfloat16 [512, 1024], replicated, may hold values from -0.25 to 0.25
- out_grad: bfloat16 [2, 8192, 1024], P('dp', 'hist'), may hold values from -6 to 6
Outputs:
- query_grad: bfloat16 [2, 8192, 512], P('dp', 'hist')
- key_grad: bfloat16 [2, 8192, 512], P('dp', 'hist')
- value_grad: bfloat16 [2, 8192, 512], P('dp', 'hist')
- gate_grad: bfloat16 [2, 8192, 512], P('dp', 'hist')
- weight_grad: float32 [512, 1024], P('hist')
The draws below stay inside these ranges and needn't reach their ends.
Inputs may be any that keep to these rules, and one draw needn't show every extreme that they name: user_start[g, i] is the position within group g of the first event of event i's user: it is at most i, never falls along the events, equals i where a user begins, and is 0 at the first event; the last event of every group is a user of its own.
All inputs are finite; a program needn't handle non-finite values.
Results may differ from the reference program's by a relative error of at most 0.012.
Values may be sent and summed in bfloat16 or wider, within the bound.
A program may use at most 128 MiB of HBM per device.

```python
import math
import jax
import jax.numpy as jnp
from jax import lax

D = 1024
HEADS = 4
HS = 128
WIN = 512
EV_DEV = 512
HD = 512
GROUPS = 2
EVENTS = 8192


def draw_user_start(key, part):
    zone_key, ticket_key = jax.random.split(jax.random.fold_in(key, 7))
    zone_count = GROUPS * EVENTS // EV_DEV
    exponent = jax.random.randint(zone_key, (zone_count, 1), 3, 13)
    period = jnp.left_shift(jnp.ones_like(exponent), exponent)
    ticket = jax.random.randint(ticket_key, (zone_count, EV_DEV), 0, 1048576)
    flags = ticket % period == 0
    flags = flags.reshape(GROUPS, EVENTS)
    position = jnp.arange(EVENTS, dtype=jnp.int32)[None, :]
    flags = flags | (position == 0) | (position == EVENTS - 1)
    marks = jnp.where(flags, position, 0).astype(jnp.int32)
    return lax.cummax(marks, axis=1).astype(jnp.int32)


def raised(drawn, key, source, target, parts, factor):
    def block_of(dim):
        return (jnp.arange(drawn.shape[dim]) // (drawn.shape[dim] // parts)).reshape((-1,) + (1,) * (drawn.ndim - 1 - dim))

    first = jax.random.permutation(key, parts)[block_of(target)]
    second = (block_of(target) + parts // 2) % parts
    return jnp.where((block_of(source) == first) | (block_of(source) == second), factor * drawn, drawn)


def shard_levels(key, extent, shards, low, high):
    factor_of, own = 1.0, jax.random.fold_in(key, 6)
    for dim, blocks in shards:
        draws = jnp.exp(jax.random.uniform(jax.random.fold_in(own, dim), (blocks,), jnp.float32, low / len(shards), high / len(shards)))
        factor_of = factor_of * jnp.repeat(draws, extent[dim] // blocks).reshape([-1 if axis == dim else 1 for axis in range(len(extent))])
    return factor_of


def scatter_about(key, extent, deviation, limit, cuts=(), kind=jnp.bfloat16):
    result = jax.random.normal(key, extent, jnp.float32) * deviation
    if len(cuts) > 0:
        result = shard_levels(key, extent, cuts, -0.22, 0.18) * result
    return jnp.clip(result, min=-limit, max=limit).astype(kind)


def gaussian_with(own_key, dims, spread, bound, cuts, heavy, kind=jnp.bfloat16):
    array = spread * jax.random.normal(own_key, dims, jnp.float32)
    if cuts:
        array = array * shard_levels(own_key, dims, cuts, -0.22, 0.18)
    return jnp.clip(raised(array, jax.random.fold_in(own_key, 3), *heavy), -bound, bound).astype(kind)


def setup_inputs(seed: int = 0) -> dict:
    key_of = jax.random.split(jax.random.key(seed), 8)
    return {
        "queries": scatter_about(key_of[0], (GROUPS, EVENTS, HD), 1.0, 6.0, ((0, 2), (1, 16))),
        "key_rows": scatter_about(key_of[1], (GROUPS, EVENTS, HD), 1.0, 6.0, ((0, 2), (1, 16))),
        "value_rows": scatter_about(key_of[2], (GROUPS, EVENTS, HD), 1.0, 6.0, ((0, 2), (1, 16))),
        "gate_rows": gaussian_with(key_of[3], (GROUPS, EVENTS, HD), 1.0, 6.0, ((0, 2), (1, 16)), (1, 2, 16, 2.0)),
        "user_start": draw_user_start(jax.random.fold_in(key_of[7], 71), 0),
        "w_out": scatter_about(key_of[5], (HD, D), HD ** -0.5, 0.25),
        "out_grad": scatter_about(key_of[6], (GROUPS, EVENTS, D), 1.0, 6.0, ((0, 2), (1, 16))),
    }


EPSILON = 1e-05

def split_heads(values):
    return values.reshape(values.shape[0], HEADS, HS)

def row_section(attended, gate_blk, grad_blk, w_out):
    row_mean = lax.optimization_barrier(jnp.mean(attended, axis=-1, keepdims=True))
    centred = attended - row_mean
    inverse = lax.rsqrt(lax.optimization_barrier(jnp.mean(centred * centred, axis=-1, keepdims=True)) + EPSILON)
    normed = centred * inverse
    gate_wide = gate_blk.astype(jnp.float32)
    hidden = (normed * gate_wide).astype(jnp.bfloat16)
    d_hidden = jnp.dot(grad_blk, w_out.T, preferred_element_type=jnp.float32)
    gate_grad = (d_hidden * normed).astype(jnp.bfloat16)
    d_normed = d_hidden * gate_wide
    d_attn = inverse * (d_normed - lax.optimization_barrier(jnp.mean(d_normed, axis=-1, keepdims=True)) - normed * lax.optimization_barrier(jnp.mean(d_normed * normed, axis=-1, keepdims=True)))
    return (hidden, gate_grad, d_attn.astype(jnp.bfloat16))

def group_pass(queries, key_rows, value_rows, gate_rows, user_start, grad_rows, w_out):
    events, width = queries.shape
    block = math.gcd(512, events)
    span = block + WIN
    front = jnp.zeros((WIN, width), queries.dtype)
    padded_keys = jnp.concatenate([front, key_rows], 0)
    padded_values = jnp.concatenate([front, value_rows], 0)
    inv_root = HS ** (-0.5)

    def step(carry, block_index):
        key_acc, value_acc, weight_acc = carry
        first = block_index * block
        query_blk = lax.dynamic_slice_in_dim(queries, first, block, 0)
        gate_blk = lax.dynamic_slice_in_dim(gate_rows, first, block, 0)
        start_blk = lax.dynamic_slice_in_dim(user_start, first, block, 0)
        grad_blk = lax.dynamic_slice_in_dim(grad_rows, first, block, 0)
        key_win = lax.dynamic_slice_in_dim(padded_keys, first, span, 0)
        value_win = lax.dynamic_slice_in_dim(padded_values, first, span, 0)
        query_pos = first + jnp.arange(block, dtype=jnp.int32)
        key_pos = first - WIN + jnp.arange(span, dtype=jnp.int32)
        spacing = query_pos[:, None] - key_pos[None, :]
        live_map = (key_pos[None, :] >= start_blk[:, None]) & (spacing >= 0) & (spacing < WIN)
        query_h = split_heads(query_blk).astype(jnp.float32)
        key_h = split_heads(key_win).astype(jnp.float32)
        value_h = split_heads(value_win).astype(jnp.float32)
        scaled = jnp.einsum('rhd,chd->hrc', query_h, key_h) * inv_root
        sigmoid_s = jax.nn.sigmoid(scaled)
        weights = jnp.where(live_map[None], scaled * sigmoid_s / WIN, 0.0).astype(jnp.bfloat16)
        weights_wide = weights.astype(jnp.float32)
        attended = jnp.einsum('hrc,chd->rhd', weights_wide, value_h).reshape(block, width)
        hidden, gate_grad, d_attn = row_section(attended, gate_blk, grad_blk, w_out)
        d_heads = split_heads(d_attn).astype(jnp.float32)
        d_weights = jnp.einsum('rhd,chd->hrc', d_heads, value_h)
        d_scores = jnp.where(live_map[None], d_weights * sigmoid_s * (1.0 + scaled * (1.0 - sigmoid_s)) / WIN, 0.0)
        d_scores = d_scores.astype(jnp.bfloat16).astype(jnp.float32)
        query_part = jnp.einsum('hrc,chd->rhd', d_scores, key_h).reshape(block, width) * inv_root
        key_part = jnp.einsum('hrc,rhd->chd', d_scores, query_h).reshape(span, width) * inv_root
        value_part = jnp.einsum('hrc,rhd->chd', weights_wide, d_heads).reshape(span, width)
        key_acc = lax.dynamic_update_slice_in_dim(key_acc, lax.dynamic_slice_in_dim(key_acc, first, span, 0) + key_part, first, 0)
        value_acc = lax.dynamic_update_slice_in_dim(value_acc, lax.dynamic_slice_in_dim(value_acc, first, span, 0) + value_part, first, 0)
        weight_acc = weight_acc + jnp.dot(hidden.T, grad_blk, preferred_element_type=jnp.float32)
        return ((key_acc, value_acc, weight_acc), (query_part.astype(jnp.bfloat16), gate_grad))
    start_carry = (jnp.zeros((events + WIN, width), jnp.float32), jnp.zeros((events + WIN, width), jnp.float32), jnp.zeros((width, w_out.shape[1]), jnp.float32))
    (key_acc, value_acc, weight_acc), (query_grads, gate_grads) = lax.scan(step, start_carry, jnp.arange(events // block, dtype=jnp.int32))
    return (query_grads.reshape(events, width), key_acc[WIN:].astype(jnp.bfloat16), value_acc[WIN:].astype(jnp.bfloat16), gate_grads.reshape(events, width), weight_acc)

def reference(queries, key_rows, value_rows, gate_rows, user_start, w_out, out_grad):

    def one_group(members):
        return group_pass(members[0], members[1], members[2], members[3], members[4], members[5], w_out)
    query_grad, key_grad, value_grad, gate_grad, weight_parts = lax.map(one_group, (queries, key_rows, value_rows, gate_rows, user_start, out_grad))
    weight_grad = lax.optimization_barrier(jnp.sum(weight_parts, axis=0)) / math.sqrt(GROUPS * EVENTS)
    return (query_grad, key_grad, value_grad, gate_grad, weight_grad)
```

```python
import functools
import math

import jax
import jax.numpy as jnp
from jax import lax
from jax.experimental import pallas as pl
from jax.experimental.pallas import tpu as pltpu
from jax.sharding import PartitionSpec as P

HEADS = 4
HS = 128
WIN = 512
EPSILON = 1e-05
BF = jnp.bfloat16
F32 = jnp.float32


def dot(a, b, ca, cb):
    return lax.dot_general(a, b, (((ca,), (cb,)), ((), ())), preferred_element_type=F32)


def kernel(
    n, dp, total_rows,
    q_ref, k_ref, v_ref, u_ref, st_ref, w_ref, go_ref,
    dq_ref, dk_ref, dv_ref, du_ref, dw_ref,
    halo, w_s, g_s, att, dh, da, hid, out_kv, in_kv, wp, *rest,
):
    steps = n.bit_length() - 1
    dsteps = dp.bit_length() - 1
    hops = steps + dsteps
    sends, recvs = rest[:hops], rest[hops : 2 * hops]
    ks, kr, gs, gr, ws, wr = rest[2 * hops :]
    ev = q_ref.shape[0]
    blk = ev // 2
    me = lax.axis_index("hist")
    mine = lax.axis_index("dp")
    has_left = me > 0
    has_right = me < n - 1
    mesh = pl.DeviceIdType.MESH

    def xor(value, bit):
        return value + bit - 2 * bit * ((value // bit) % 2)

    partners = [{"hist": xor(me, 1 << s)} for s in range(steps)]
    partners += [{"dp": xor(mine, 1 << s)} for s in range(dsteps)]

    barrier = pltpu.get_barrier_semaphore()
    for partner in partners:
        pl.semaphore_signal(barrier, inc=1, device_id=partner, device_id_type=mesh)

    @pl.when(has_right)
    def _():
        pl.semaphore_signal(barrier, inc=1, device_id={"hist": me + 1}, device_id_type=mesh)

    @pl.when(has_left)
    def _():
        pl.semaphore_signal(barrier, inc=1, device_id={"hist": me - 1}, device_id_type=mesh)

    pl.semaphore_wait(barrier, hops + has_left.astype(jnp.int32) + has_right.astype(jnp.int32))

    halo_copies = [
        pltpu.make_async_remote_copy(
            src_ref=ref, dst_ref=halo.at[i], send_sem=ks.at[i], recv_sem=kr.at[i],
            device_id={"hist": me + 1}, device_id_type=mesh,
        )
        for i, ref in enumerate((k_ref, v_ref))
    ]
    grad_copies = [
        pltpu.make_async_remote_copy(
            src_ref=out_kv.at[h], dst_ref=in_kv.at[h], send_sem=gs.at[h], recv_sem=gr.at[h],
            device_id={"hist": me - 1}, device_id_type=mesh,
        )
        for h in range(HEADS)
    ]
    sum_copies = [
        pltpu.make_async_remote_copy(
            src_ref=sends[s], dst_ref=recvs[s], send_sem=ws.at[s], recv_sem=wr.at[s],
            device_id=partners[s], device_id_type=mesh,
        )
        for s in range(hops)
    ]

    @pl.when(has_right)
    def _():
        for copy in halo_copies:
            copy.start()

    @pl.when(me == 0)
    def _():
        halo[...] = jnp.zeros_like(halo)

    @pl.when(me == n - 1)
    def _():
        in_kv[...] = jnp.zeros_like(in_kv)

    scale = HS ** (-0.5)
    base = me * ev

    def head(h):
        return slice(h * HS, (h + 1) * HS)

    def mask(part, b, lo, hi):
        cols = slice(b * blk, (b + 1) * blk)
        start = st_ref[:, cols] - base
        jj = lax.broadcasted_iota(jnp.int32, (hi - lo, blk), 0) + lo
        ii = lax.broadcasted_iota(jnp.int32, (hi - lo, blk), 1) + b * blk
        if part == 0:
            live = (jj >= start + ev) & (jj > ii)
        else:
            live = (jj >= start) & (jj <= ii)
        return jnp.where(live, 1.0 / WIN, 0.0).astype(F32)

    def span(part, b):
        return (b * blk, ev) if part == 0 else (0, (b + 1) * blk)

    def scores(part, b, h, keys, live):
        lo, hi = span(part, b)
        cols = slice(b * blk, (b + 1) * blk)
        x = dot(keys[lo:hi, head(h)], q_ref[cols, head(h)], 1, 1) * scale
        sig = 0.5 * jnp.tanh(0.5 * x) + 0.5
        part_sig = sig * live
        wt = x * part_sig
        g_s[h, part, lo:hi, cols] = (part_sig + wt * (1.0 - sig)).astype(BF)
        w_s[h, part, lo:hi, cols] = wt.astype(BF)

    def mix(part, b, h, values):
        lo, hi = span(part, b)
        cols = slice(b * blk, (b + 1) * blk)
        return dot(w_s[h, part, lo:hi, cols], values[lo:hi, head(h)], 0, 0)

    for b in range(2):
        live = mask(1, b, *span(1, b))
        for h in range(HEADS):
            scores(1, b, h, k_ref, live)
            att[b * blk : (b + 1) * blk, head(h)] = mix(1, b, h, v_ref)
    for b in range(2):
        rows = slice(b * blk, (b + 1) * blk)
        dh[rows, :] = dot(go_ref[rows, :], w_ref[...], 1, 1)

    @pl.when(has_left)
    def _():
        halo_copies[0].wait_recv()

    for b in range(2):
        live = mask(0, b, *span(0, b))
        for h in range(HEADS):
            scores(0, b, h, halo.at[0], live)

    @pl.when(has_left)
    def _():
        halo_copies[1].wait_recv()

    for b in range(2):
        for h in range(HEADS):
            att[b * blk : (b + 1) * blk, head(h)] += mix(0, b, h, halo.at[1])

    chunk = 64
    @pl.loop(0, ev // chunk)
    def _(c):
        rows = pl.ds(pl.multiple_of(c * chunk, chunk), chunk)
        a = att[rows, :]
        centred = a - jnp.mean(a, axis=-1, keepdims=True)
        inverse = lax.rsqrt(jnp.mean(centred * centred, axis=-1, keepdims=True) + EPSILON)
        normed = centred * inverse
        gate = u_ref[rows, :].astype(F32)
        hid[rows, :] = (normed * gate).astype(BF)
        d_hidden = dh[rows, :]
        du_ref[rows, :] = (d_hidden * normed).astype(BF)
        d_normed = d_hidden * gate
        d_attn = inverse * (
            d_normed
            - jnp.mean(d_normed, axis=-1, keepdims=True)
            - normed * jnp.mean(d_normed * normed, axis=-1, keepdims=True)
        )
        da[rows, :] = d_attn.astype(BF)

    block_rows = wp.shape[1]

    def weight_part():
        cols = hid.shape[1] // 2
        for b in range(2):
            piece = dot(hid[:, b * cols : (b + 1) * cols], go_ref[...], 0, 0)
            wp[b * n // 2 : (b + 1) * n // 2] = piece.reshape(n // 2, block_rows, piece.shape[1])

    def launch(s):
        if s < steps:
            count = n >> (s + 1)
            bit = (me // (1 << s)) % 2
            for i in range(count):
                sends[s][i] = wp[2 * i + 1 - bit].astype(BF)
        else:
            sends[s][0] = wp[0].astype(BF)
        sum_copies[s].start()

    def land(s):
        sum_copies[s].wait_recv()
        if s < steps:
            count = n >> (s + 1)
            bit = (me // (1 << s)) % 2
            for i in range(count):
                wp[i] = wp[2 * i + bit] + recvs[s][i].astype(F32)
        else:
            wp[0] = sends[s][0].astype(F32) + recvs[s][0].astype(F32)

    def queries(part, kb):
        return slice(0, (kb + 1) * blk) if part == 0 else slice(kb * blk, ev)

    def back(part, h, keep):
        values = halo.at[1] if part == 0 else v_ref
        for kb in range(2):
            rows = slice(kb * blk, (kb + 1) * blk)
            cols = queries(part, kb)
            d_rows = da[cols, head(h)]
            d_w = dot(values[rows, head(h)], d_rows, 1, 1)
            d_s = (d_w * g_s[h, part, rows, cols].astype(F32)).astype(BF)
            g_s[h, part, rows, cols] = d_s
            d_k = dot(d_s, q_ref[cols, head(h)], 1, 0) * scale
            d_v = dot(w_s[h, part, rows, cols], d_rows, 1, 0)
            keep(h, rows, d_k, d_v)

    def keep_far(h, rows, d_k, d_v):
        out_kv[h, 0, rows, :] = d_k.astype(BF)
        out_kv[h, 1, rows, :] = d_v.astype(BF)

    def far(h):
        back(0, h, keep_far)

        @pl.when(has_left)
        def _():
            grad_copies[h].start()

    def keep_near(h, rows, d_k, d_v):
        att[rows, head(h)] = d_k
        dh[rows, head(h)] = d_v

    def near(h):
        back(1, h, keep_near)

    def query_side(h):
        for b in range(2):
            cols = slice(b * blk, (b + 1) * blk)
            total = 0.0
            for part, keys in ((0, halo.at[0]), (1, k_ref)):
                lo, hi = span(part, b)
                total = total + dot(g_s[h, part, lo:hi, cols], keys[lo:hi, head(h)], 0, 0)
            dq_ref[cols, head(h)] = (total * scale).astype(BF)

    def finish(h):
        @pl.when(has_right)
        def _():
            grad_copies[h].wait_recv()

        dk_ref[:, head(h)] = (att[:, head(h)] + in_kv[h, 0].astype(F32)).astype(BF)
        dv_ref[:, head(h)] = (dh[:, head(h)] + in_kv[h, 1].astype(F32)).astype(BF)

    weight_part()
    launch(0)
    work = [(far, 0), (far, 1), (far, 2), (far, 3)]
    work += [(near, 0), (near, 1), (near, 2), (near, 3)]
    work += [(query_side, 0), (query_side, 1), (query_side, 2), (query_side, 3)]
    pending = 0
    for i, (task, h) in enumerate(work):
        task(h)
        if i % 3 == 2 or i == 1:
            if pending < hops - 1:
                land(pending)
                pending += 1
                launch(pending)
    while pending < hops - 1:
        land(pending)
        pending += 1
        launch(pending)
    for h in range(HEADS):
        finish(h)
    land(hops - 1)
    dw_ref[...] = wp[0] / math.sqrt(total_rows)

    @pl.when(has_right)
    def _():
        for copy in halo_copies:
            copy.wait_send()

    @pl.when(has_left)
    def _():
        for copy in grad_copies:
            copy.wait_send()

    for copy in sum_copies:
        copy.wait_send()


def shards(n, dp, queries, key_rows, value_rows, gate_rows, user_start, w_out, out_grad):
    ev, width = queries.shape[1:]
    model = w_out.shape[1]
    block_rows = width // n
    steps = n.bit_length() - 1
    dsteps = dp.bit_length() - 1
    hops = steps + dsteps
    sizes = [n >> (s + 1) for s in range(steps)] + [1] * dsteps
    legs = [pltpu.VMEM((size, block_rows, model), BF) for size in sizes]
    rows = jax.ShapeDtypeStruct((ev, width), BF)
    vmem = pl.BlockSpec(memory_space=pltpu.VMEM)
    dma = pltpu.SemaphoreType.DMA
    results = pl.pallas_call(
        functools.partial(kernel, n, dp, dp * n * ev),
        out_shape=(rows, rows, rows, rows, jax.ShapeDtypeStruct((block_rows, model), F32)),
        in_specs=[vmem] * 7,
        out_specs=(vmem,) * 5,
        scratch_shapes=[
            pltpu.VMEM((2, ev, width), BF),
            pltpu.VMEM((HEADS, 2, ev, ev), BF),
            pltpu.VMEM((HEADS, 2, ev, ev), BF),
            pltpu.VMEM((ev, width), F32),
            pltpu.VMEM((ev, width), F32),
            pltpu.VMEM((ev, width), BF),
            pltpu.VMEM((ev, width), BF),
            pltpu.VMEM((HEADS, 2, ev, HS), BF),
            pltpu.VMEM((HEADS, 2, ev, HS), BF),
            pltpu.VMEM((n, block_rows, model), F32),
        ]
        + legs
        + legs
        + [dma((2,)), dma((2,)), dma((HEADS,)), dma((HEADS,)), dma((hops,)), dma((hops,))],
        compiler_params=pltpu.CompilerParams(
            collective_id=0, has_side_effects=True, vmem_limit_bytes=60 * 1024 * 1024
        ),
    )(
        queries[0], key_rows[0], value_rows[0], gate_rows[0], user_start, w_out, out_grad[0]
    )
    return tuple(r[None] for r in results[:4]) + (results[4],)


def solution(mesh):
    n, dp = mesh.shape["hist"], mesh.shape["dp"]
    return jax.shard_map(
        functools.partial(shards, n, dp),
        mesh=mesh,
        in_specs=(
            P("dp", "hist", None),
            P("dp", "hist", None),
            P("dp", "hist", None),
            P("dp", "hist", None),
            P("dp", "hist"),
            P(),
            P("dp", "hist", None),
        ),
        out_specs=(
            P("dp", "hist", None),
            P("dp", "hist", None),
            P("dp", "hist", None),
            P("dp", "hist", None),
            P("hist", None),
        ),
        check_vma=False,
    )
```

```python
import functools
import math

import jax
import jax.numpy as jnp
from jax import lax
from jax.experimental import pallas as pl
from jax.experimental.pallas import tpu as pltpu
from jax.sharding import PartitionSpec as P

HEADS = 4
HS = 128
WIN = 512
EPSILON = 1e-05
BF = jnp.bfloat16
F32 = jnp.float32


def dot(a, b, ca, cb):
    return lax.dot_general(a, b, (((ca,), (cb,)), ((), ())), preferred_element_type=F32)


def routes(n, dp):
    steps, dsteps = n.bit_length() - 1, dp.bit_length() - 1
    plans = []
    for at in (1, 2):
        plan, split = [], False
        for s in range(steps):
            if s == at:
                plan.append(("split", 0, n >> s, True))
                split = True
            plan.append(("hist", s, n >> (s + 1), split))
        plan += [("both", s, 1, True) for s in range(1, dsteps)]
        plan.append(("gather", 0, 1, True))
        plans.append(plan)
    return plans


def kernel(
    n, dp, total_rows,
    st_ref, q_hbm, k_hbm, v_hbm, u_hbm, w_hbm, go_hbm,
    dq_ref, dk_ref, dv_ref, du_ref, dw_ref,
    q_ref, k_ref, v_ref, u_ref, w_ref, go_ref, in_sem,
    halo, w_s, g_s, att, dh, da, hid, out_kv, in_kv, wp, *rest,
):
    steps = n.bit_length() - 1
    dsteps = dp.bit_length() - 1
    plans = routes(n, dp)
    hops = len(plans[0])
    count = 2 * hops
    sends = (rest[:hops], rest[hops:count])
    recvs = (rest[count : count + hops], rest[count + hops : 2 * count])
    ks, kr, gs, gr, ws, wr = rest[2 * count :]
    loads = [
        pltpu.make_async_copy(src, dst, in_sem.at[i])
        for i, (src, dst) in enumerate(
            (
                (k_hbm, k_ref),
                (q_hbm, q_ref),
                (v_hbm, v_ref),
                (w_hbm, w_ref),
                (go_hbm, go_ref),
                (u_hbm, u_ref),
            )
        )
    ]
    for load in loads:
        load.start()
    ev = q_ref.shape[0]
    blk = ev // 2
    me = lax.axis_index("hist")
    mine = lax.axis_index("dp")
    has_left = me > 0
    has_right = me < n - 1
    mesh = pl.DeviceIdType.MESH

    def xor(value, bit):
        return value + bit - 2 * bit * ((value // bit) % 2)

    hist_partners = [{"hist": xor(me, 1 << s)} for s in range(steps)]
    dp_partners = [{"dp": xor(mine, 1 << s)} for s in range(dsteps)]
    partners = hist_partners + dp_partners

    barrier = pltpu.get_barrier_semaphore()
    for partner in partners:
        pl.semaphore_signal(barrier, inc=1, device_id=partner, device_id_type=mesh)

    @pl.when(has_right)
    def _():
        pl.semaphore_signal(barrier, inc=1, device_id={"hist": me + 1}, device_id_type=mesh)

    @pl.when(has_left)
    def _():
        pl.semaphore_signal(barrier, inc=1, device_id={"hist": me - 1}, device_id_type=mesh)

    pl.semaphore_wait(barrier, steps + dsteps + has_left.astype(jnp.int32) + has_right.astype(jnp.int32))

    halo_copies = [
        pltpu.make_async_remote_copy(
            src_ref=ref, dst_ref=halo.at[i], send_sem=ks.at[i], recv_sem=kr.at[i],
            device_id={"hist": me + 1}, device_id_type=mesh,
        )
        for i, ref in enumerate((k_hbm, v_hbm))
    ]
    grad_copies = [
        pltpu.make_async_remote_copy(
            src_ref=out_kv.at[h], dst_ref=in_kv.at[h], send_sem=gs.at[h], recv_sem=gr.at[h],
            device_id={"hist": me - 1}, device_id_type=mesh,
        )
        for h in range(HEADS)
    ]
    sum_copies = [
        [
            pltpu.make_async_remote_copy(
                src_ref=sends[c][i], dst_ref=recvs[c][i],
                send_sem=ws.at[c * hops + i], recv_sem=wr.at[c * hops + i],
                device_id=(hist_partners if kind == "hist" else dp_partners)[s],
                device_id_type=mesh,
            )
            for i, (kind, s, _, _) in enumerate(plans[c])
        ]
        for c in range(2)
    ]

    @pl.when(has_right)
    def _():
        for copy in halo_copies:
            copy.start()

    @pl.when(me == 0)
    def _():
        halo[...] = jnp.zeros_like(halo)

    @pl.when(me == n - 1)
    def _():
        in_kv[...] = jnp.zeros_like(in_kv)

    scale = HS ** (-0.5)
    base = me * ev

    def head(h):
        return slice(h * HS, (h + 1) * HS)

    def mask(part, b, lo, hi):
        cols = slice(b * blk, (b + 1) * blk)
        start = st_ref[:, cols] - base
        jj = lax.broadcasted_iota(jnp.int32, (hi - lo, blk), 0) + lo
        ii = lax.broadcasted_iota(jnp.int32, (hi - lo, blk), 1) + b * blk
        if part == 0:
            live = (jj >= start + ev) & (jj > ii)
        else:
            live = (jj >= start) & (jj <= ii)
        return jnp.where(live, 1.0 / WIN, 0.0).astype(F32)

    def span(part, b):
        return (b * blk, ev) if part == 0 else (0, (b + 1) * blk)

    def scores(part, b, h, keys, live):
        lo, hi = span(part, b)
        cols = slice(b * blk, (b + 1) * blk)
        x = dot(keys[lo:hi, head(h)], q_ref[cols, head(h)], 1, 1) * scale
        sig = 0.5 * jnp.tanh(0.5 * x) + 0.5
        part_sig = sig * live
        wt = x * part_sig
        g_s[h, part, lo:hi, cols] = (part_sig + wt * (1.0 - sig)).astype(BF)
        w_s[h, part, lo:hi, cols] = wt.astype(BF)

    def mix(part, b, h, values):
        lo, hi = span(part, b)
        cols = slice(b * blk, (b + 1) * blk)
        return dot(w_s[h, part, lo:hi, cols], values[lo:hi, head(h)], 0, 0)

    for load in loads[:3]:
        load.wait()
    for b in range(2):
        live = mask(1, b, *span(1, b))
        for h in range(HEADS):
            scores(1, b, h, k_ref, live)
            att[b * blk : (b + 1) * blk, head(h)] = mix(1, b, h, v_ref)
    for load in loads[3:]:
        load.wait()
    for b in range(2):
        rows = slice(b * blk, (b + 1) * blk)
        dh[rows, :] = dot(go_ref[rows, :], w_ref[...], 1, 1)

    @pl.when(has_left)
    def _():
        halo_copies[0].wait_recv()

    for b in range(2):
        live = mask(0, b, *span(0, b))
        for h in range(HEADS):
            scores(0, b, h, halo.at[0], live)

    @pl.when(has_left)
    def _():
        halo_copies[1].wait_recv()

    for b in range(2):
        for h in range(HEADS):
            att[b * blk : (b + 1) * blk, head(h)] += mix(0, b, h, halo.at[1])

    chunk = 64
    @pl.loop(0, ev // chunk)
    def _(c):
        rows = pl.ds(pl.multiple_of(c * chunk, chunk), chunk)
        a = att[rows, :]
        centred = a - jnp.mean(a, axis=-1, keepdims=True)
        inverse = lax.rsqrt(jnp.mean(centred * centred, axis=-1, keepdims=True) + EPSILON)
        normed = centred * inverse
        gate = u_ref[rows, :].astype(F32)
        hid[rows, :] = (normed * gate).astype(BF)
        d_hidden = dh[rows, :]
        du_ref[rows, :] = (d_hidden * normed).astype(BF)
        d_normed = d_hidden * gate
        d_attn = inverse * (
            d_normed
            - jnp.mean(d_normed, axis=-1, keepdims=True)
            - normed * jnp.mean(d_normed * normed, axis=-1, keepdims=True)
        )
        da[rows, :] = d_attn.astype(BF)

    block_rows = wp.shape[2]
    width = wp.shape[3]
    low = mine % 2

    def weight_part():
        for g in range(4):
            piece = dot(hid[...], go_ref[:, g * width : (g + 1) * width], 0, 0)
            wp[g] = piece.reshape(n, block_rows, width)

    def groups(c, split):
        return [2 * c + low] if split else [2 * c, 2 * c + 1]

    def launch(c, i):
        kind, s, size, split = plans[c][i]
        target = sends[c][i]
        if kind == "hist":
            bit = (me // (1 << s)) % 2
            for a, g in enumerate(groups(c, split)):
                for j in range(size):
                    target[a, j] = wp[g, 2 * j + 1 - bit].astype(BF)
        elif kind == "split":
            for j in range(size):
                target[0, j] = wp[2 * c + 1 - low, j].astype(BF)
        else:
            target[0, 0] = wp[2 * c + low, 0].astype(BF)
        sum_copies[c][i].start()

    def land(c, i):
        kind, s, size, split = plans[c][i]
        source = recvs[c][i]
        sum_copies[c][i].wait_recv()
        if kind == "hist":
            bit = (me // (1 << s)) % 2
            for a, g in enumerate(groups(c, split)):
                for j in range(size):
                    wp[g, j] = wp[g, 2 * j + bit] + source[a, j].astype(F32)
        elif kind == "split":
            for j in range(size):
                wp[2 * c + low, j] = wp[2 * c + low, j] + source[0, j].astype(F32)
        elif kind == "both":
            wp[2 * c + low, 0] = sends[c][i][0, 0].astype(F32) + source[0, 0].astype(F32)
        else:
            wp[2 * c + low, 0] = sends[c][i][0, 0].astype(F32)
            wp[2 * c + 1 - low, 0] = source[0, 0].astype(F32)

    def queries(part, kb):
        return slice(0, (kb + 1) * blk) if part == 0 else slice(kb * blk, ev)

    def back(part, h, keep):
        values = halo.at[1] if part == 0 else v_ref
        for kb in range(2):
            rows = slice(kb * blk, (kb + 1) * blk)
            cols = queries(part, kb)
            d_rows = da[cols, head(h)]
            d_w = dot(values[rows, head(h)], d_rows, 1, 1)
            d_s = (d_w * g_s[h, part, rows, cols].astype(F32)).astype(BF)
            g_s[h, part, rows, cols] = d_s
            d_k = dot(d_s, q_ref[cols, head(h)], 1, 0) * scale
            d_v = dot(w_s[h, part, rows, cols], d_rows, 1, 0)
            keep(h, rows, d_k, d_v)

    def keep_far(h, rows, d_k, d_v):
        out_kv[h, 0, rows, :] = d_k.astype(BF)
        out_kv[h, 1, rows, :] = d_v.astype(BF)

    def far(h):
        back(0, h, keep_far)

        @pl.when(has_left)
        def _():
            grad_copies[h].start()

    def keep_near(h, rows, d_k, d_v):
        att[rows, head(h)] = d_k
        dh[rows, head(h)] = d_v

    def near(h):
        back(1, h, keep_near)

    def query_side(h):
        for b in range(2):
            cols = slice(b * blk, (b + 1) * blk)
            total = 0.0
            for part, keys in ((0, halo.at[0]), (1, k_ref)):
                lo, hi = span(part, b)
                total = total + dot(g_s[h, part, lo:hi, cols], keys[lo:hi, head(h)], 0, 0)
            dq_ref[cols, head(h)] = (total * scale).astype(BF)

    def finish(h):
        @pl.when(has_right)
        def _():
            grad_copies[h].wait_recv()

        dk_ref[:, head(h)] = (att[:, head(h)] + in_kv[h, 0].astype(F32)).astype(BF)
        dv_ref[:, head(h)] = (dh[:, head(h)] + in_kv[h, 1].astype(F32)).astype(BF)

    pending = 0

    def advance():
        nonlocal pending
        if pending < hops - 1:
            for c in range(2):
                land(c, pending)
                launch(c, pending + 1)
            pending += 1

    weight_part()
    launch(0, 0)
    launch(1, 0)
    far(0)
    advance()
    far(1)
    far(2)
    far(3)
    advance()
    near(0)
    near(1)
    advance()
    near(2)
    near(3)
    advance()
    for h in range(HEADS):
        query_side(h)
        if h == 2:
            advance()
    while pending < hops - 1:
        advance()
    for h in range(HEADS):
        finish(h)
    root = math.sqrt(total_rows)
    for c in range(2):
        land(c, hops - 1)
        for g in (2 * c, 2 * c + 1):
            dw_ref[:, g * width : (g + 1) * width] = wp[g, 0] / root

    @pl.when(has_right)
    def _():
        for copy in halo_copies:
            copy.wait_send()

    @pl.when(has_left)
    def _():
        for copy in grad_copies:
            copy.wait_send()

    for copies in sum_copies:
        for copy in copies:
            copy.wait_send()


def emit(*refs):
    sems = refs[10]
    copies = [pltpu.make_async_copy(refs[i], refs[5 + i], sems.at[i]) for i in range(5)]
    for copy in copies:
        copy.start()
    for copy in copies:
        copy.wait()


def shards(n, dp, queries, key_rows, value_rows, gate_rows, user_start, w_out, out_grad):
    ev, width = queries.shape[1:]
    model = w_out.shape[1]
    block_rows = width // n
    plans = routes(n, dp)
    hops = len(plans[0])
    legs = [
        pltpu.VMEM((1 if split else 2, size, block_rows, model // 4), BF)
        for plan in plans
        for _, _, size, split in plan
    ]
    rows = pltpu.VMEM((ev, width), BF)
    outs = (rows, rows, rows, rows, pltpu.VMEM((block_rows, model), F32))
    vmem = pl.BlockSpec(memory_space=pltpu.VMEM)
    dma = pltpu.SemaphoreType.DMA
    results = pl.pallas_call(
        functools.partial(kernel, n, dp, dp * n * ev),
        out_shape=outs,
        in_specs=[vmem] + [pl.BlockSpec(memory_space=pl.ANY)] * 6,
        out_specs=(vmem,) * 5,
        scratch_shapes=[
            pltpu.VMEM((ev, width), BF),
            pltpu.VMEM((ev, width), BF),
            pltpu.VMEM((ev, width), BF),
            pltpu.VMEM((ev, width), BF),
            pltpu.VMEM((width, model), BF),
            pltpu.VMEM((ev, model), BF),
            dma((6,)),
            pltpu.VMEM((2, ev, width), BF),
            pltpu.VMEM((HEADS, 2, ev, ev), BF),
            pltpu.VMEM((HEADS, 2, ev, ev), BF),
            pltpu.VMEM((ev, width), F32),
            pltpu.VMEM((ev, width), F32),
            pltpu.VMEM((ev, width), BF),
            pltpu.VMEM((ev, width), BF),
            pltpu.VMEM((HEADS, 2, ev, HS), BF),
            pltpu.VMEM((HEADS, 2, ev, HS), BF),
            pltpu.VMEM((4, n, block_rows, model // 4), F32),
        ]
        + legs
        + legs
        + [dma((2,)), dma((2,)), dma((HEADS,)), dma((HEADS,)), dma((2 * hops,)), dma((2 * hops,))],
        compiler_params=pltpu.CompilerParams(
            collective_id=0, has_side_effects=True, vmem_limit_bytes=60 * 1024 * 1024
        ),
    )(
        user_start, queries[0], key_rows[0], value_rows[0], gate_rows[0], w_out, out_grad[0]
    )
    results = pl.pallas_call(
        emit,
        out_shape=tuple(jax.ShapeDtypeStruct(o.shape, o.dtype) for o in outs),
        in_specs=[vmem] * 5,
        out_specs=(pl.BlockSpec(memory_space=pl.ANY),) * 5,
        scratch_shapes=[dma((5,))],
    )(*[pltpu.with_memory_space_constraint(r, pltpu.VMEM) for r in results])
    return tuple(r[None] for r in results[:4]) + (results[4],)


def solution(mesh):
    n, dp = mesh.shape["hist"], mesh.shape["dp"]
    return jax.shard_map(
        functools.partial(shards, n, dp),
        mesh=mesh,
        in_specs=(
            P("dp", "hist", None),
            P("dp", "hist", None),
            P("dp", "hist", None),
            P("dp", "hist", None),
            P("dp", "hist"),
            P(),
            P("dp", "hist", None),
        ),
        out_specs=(
            P("dp", "hist", None),
            P("dp", "hist", None),
            P("dp", "hist", None),
            P("dp", "hist", None),
            P("hist", None),
        ),
        check_vma=False,
    )
```

```python
import functools
import math

import jax
import jax.numpy as jnp
from jax import lax
from jax.experimental import pallas as pl
from jax.experimental.pallas import tpu as pltpu
from jax.sharding import PartitionSpec as P

HEADS = 4
HS = 128
WIN = 512
EPSILON = 1e-05
BF = jnp.bfloat16
F32 = jnp.float32


def dot(a, b, ca, cb):
    return lax.dot_general(a, b, (((ca,), (cb,)), ((), ())), preferred_element_type=F32)


def routes(n, dp):
    steps, dsteps = n.bit_length() - 1, dp.bit_length() - 1
    plans = []
    for at in (1, 2):
        plan, split = [], False
        for s in range(steps):
            if s == at:
                plan.append(("split", 0, n >> s, True))
                split = True
            plan.append(("hist", s, n >> (s + 1), split))
        plan += [("both", s, 1, True) for s in range(1, dsteps)]
        plan.append(("gather", 0, 1, True))
        plans.append(plan)
    return plans


def kernel(
    n, dp, total_rows,
    st_ref, q_hbm, k_hbm, v_hbm, u_hbm, w_hbm, go_hbm,
    dq_ref, dk_ref, dv_ref, du_ref, dw_ref,
    q_ref, k_ref, v_ref, u_ref, w_ref, go_ref, in_sem,
    halo, w_s, g_s, att, dh, da, hid, out_kv, in_kv, wp, *rest,
):
    steps = n.bit_length() - 1
    dsteps = dp.bit_length() - 1
    plans = routes(n, dp)
    hops = len(plans[0])
    count = 2 * hops
    sends = (rest[:hops], rest[hops:count])
    recvs = (rest[count : count + hops], rest[count + hops : 2 * count])
    ks, kr, gs, gr, ws, wr = rest[2 * count :]
    loads = [
        pltpu.make_async_copy(src, dst, in_sem.at[i])
        for i, (src, dst) in enumerate(
            (
                (k_hbm, k_ref),
                (q_hbm, q_ref),
                (v_hbm, v_ref),
                (w_hbm, w_ref),
                (go_hbm, go_ref),
                (u_hbm, u_ref),
            )
        )
    ]
    for load in loads:
        load.start()
    ev = q_ref.shape[0]
    blk = ev // 2
    me = lax.axis_index("hist")
    mine = lax.axis_index("dp")
    has_left = me > 0
    has_right = me < n - 1
    mesh = pl.DeviceIdType.MESH

    def xor(value, bit):
        return value + bit - 2 * bit * ((value // bit) % 2)

    hist_partners = [{"hist": xor(me, 1 << s)} for s in range(steps)]
    dp_partners = [{"dp": xor(mine, 1 << s)} for s in range(dsteps)]
    partners = hist_partners + dp_partners

    barrier = pltpu.get_barrier_semaphore()
    for partner in partners:
        pl.semaphore_signal(barrier, inc=1, device_id=partner, device_id_type=mesh)

    @pl.when(has_right)
    def _():
        pl.semaphore_signal(barrier, inc=1, device_id={"hist": me + 1}, device_id_type=mesh)

    @pl.when(has_left)
    def _():
        pl.semaphore_signal(barrier, inc=1, device_id={"hist": me - 1}, device_id_type=mesh)

    pl.semaphore_wait(barrier, steps + dsteps + has_left.astype(jnp.int32) + has_right.astype(jnp.int32))

    halo_copies = [
        pltpu.make_async_remote_copy(
            src_ref=ref, dst_ref=halo.at[i], send_sem=ks.at[i], recv_sem=kr.at[i],
            device_id={"hist": me + 1}, device_id_type=mesh,
        )
        for i, ref in enumerate((k_hbm, v_hbm))
    ]
    grad_copies = [
        pltpu.make_async_remote_copy(
            src_ref=out_kv.at[h], dst_ref=in_kv.at[h], send_sem=gs.at[h], recv_sem=gr.at[h],
            device_id={"hist": me - 1}, device_id_type=mesh,
        )
        for h in range(HEADS)
    ]
    sum_copies = [
        [
            pltpu.make_async_remote_copy(
                src_ref=sends[c][i], dst_ref=recvs[c][i],
                send_sem=ws.at[c * hops + i], recv_sem=wr.at[c * hops + i],
                device_id=(hist_partners if kind == "hist" else dp_partners)[s],
                device_id_type=mesh,
            )
            for i, (kind, s, _, _) in enumerate(plans[c])
        ]
        for c in range(2)
    ]

    @pl.when(has_right)
    def _():
        for copy in halo_copies:
            copy.start()

    @pl.when(me == 0)
    def _():
        halo[...] = jnp.zeros_like(halo)

    @pl.when(me == n - 1)
    def _():
        in_kv[...] = jnp.zeros_like(in_kv)

    scale = HS ** (-0.5)
    base = me * ev

    def head(h):
        return slice(h * HS, (h + 1) * HS)

    def mask(part, b, lo, hi):
        cols = slice(b * blk, (b + 1) * blk)
        start = st_ref[:, cols] - base
        jj = lax.broadcasted_iota(jnp.int32, (hi - lo, blk), 0) + lo
        ii = lax.broadcasted_iota(jnp.int32, (hi - lo, blk), 1) + b * blk
        if part == 0:
            live = (jj >= start + ev) & (jj > ii)
        else:
            live = (jj >= start) & (jj <= ii)
        return jnp.where(live, 1.0 / WIN, 0.0).astype(F32)

    def span(part, b):
        return (b * blk, ev) if part == 0 else (0, (b + 1) * blk)

    def scores(part, b, h, keys, live):
        lo, hi = span(part, b)
        cols = slice(b * blk, (b + 1) * blk)
        x = dot(keys[lo:hi, head(h)], q_ref[cols, head(h)], 1, 1) * scale
        sig = 0.5 * jnp.tanh(0.5 * x) + 0.5
        part_sig = sig * live
        wt = x * part_sig
        g_s[h, part, lo:hi, cols] = (part_sig + wt * (1.0 - sig)).astype(BF)
        w_s[h, part, lo:hi, cols] = wt.astype(BF)

    def mix(part, b, h, values):
        lo, hi = span(part, b)
        cols = slice(b * blk, (b + 1) * blk)
        return dot(w_s[h, part, lo:hi, cols], values[lo:hi, head(h)], 0, 0)

    for load in loads[:3]:
        load.wait()
    for b in range(2):
        live = mask(1, b, *span(1, b))
        for h in range(HEADS):
            scores(1, b, h, k_ref, live)
            att[b * blk : (b + 1) * blk, head(h)] = mix(1, b, h, v_ref)
    for load in loads[3:]:
        load.wait()
    for b in range(2):
        rows = slice(b * blk, (b + 1) * blk)
        dh[rows, :] = dot(go_ref[rows, :], w_ref[...], 1, 1)

    @pl.when(has_left)
    def _():
        halo_copies[0].wait_recv()

    for b in range(2):
        live = mask(0, b, *span(0, b))
        for h in range(HEADS):
            scores(0, b, h, halo.at[0], live)

    @pl.when(has_left)
    def _():
        halo_copies[1].wait_recv()

    for b in range(2):
        for h in range(HEADS):
            att[b * blk : (b + 1) * blk, head(h)] += mix(0, b, h, halo.at[1])

    chunk = 128
    @pl.loop(0, ev // chunk)
    def _(c):
        rows = pl.ds(pl.multiple_of(c * chunk, chunk), chunk)
        a = att[rows, :]
        centred = a - jnp.mean(a, axis=-1, keepdims=True)
        inverse = lax.rsqrt(jnp.mean(centred * centred, axis=-1, keepdims=True) + EPSILON)
        normed = centred * inverse
        gate = u_ref[rows, :].astype(F32)
        hid[rows, :] = (normed * gate).astype(BF)
        d_hidden = dh[rows, :]
        du_ref[rows, :] = (d_hidden * normed).astype(BF)
        d_normed = d_hidden * gate
        d_attn = inverse * (
            d_normed
            - jnp.mean(d_normed, axis=-1, keepdims=True)
            - normed * jnp.mean(d_normed * normed, axis=-1, keepdims=True)
        )
        da[rows, :] = d_attn.astype(BF)

    block_rows = wp.shape[2]
    width = wp.shape[3]
    low = mine % 2

    def weight_part():
        whole = dot(hid[...], go_ref[...], 0, 0)
        for g in range(4):
            wp[g] = whole[:, g * width : (g + 1) * width].reshape(n, block_rows, width)

    def groups(c, split):
        return [2 * c + low] if split else [2 * c, 2 * c + 1]

    def launch(c, i):
        kind, s, size, split = plans[c][i]
        target = sends[c][i]
        if kind == "hist":
            bit = (me // (1 << s)) % 2
            for a, g in enumerate(groups(c, split)):
                for j in range(size):
                    target[a, j] = wp[g, 2 * j + 1 - bit].astype(BF)
        elif kind == "split":
            for j in range(size):
                target[0, j] = wp[2 * c + 1 - low, j].astype(BF)
        else:
            target[0, 0] = wp[2 * c + low, 0].astype(BF)
        sum_copies[c][i].start()

    def land(c, i):
        kind, s, size, split = plans[c][i]
        source = recvs[c][i]
        sum_copies[c][i].wait_recv()
        if kind == "hist":
            bit = (me // (1 << s)) % 2
            for a, g in enumerate(groups(c, split)):
                for j in range(size):
                    wp[g, j] = wp[g, 2 * j + bit] + source[a, j].astype(F32)
        elif kind == "split":
            for j in range(size):
                wp[2 * c + low, j] = wp[2 * c + low, j] + source[0, j].astype(F32)
        elif kind == "both":
            wp[2 * c + low, 0] = sends[c][i][0, 0].astype(F32) + source[0, 0].astype(F32)
        else:
            wp[2 * c + low, 0] = sends[c][i][0, 0].astype(F32)
            wp[2 * c + 1 - low, 0] = source[0, 0].astype(F32)

    def queries(part, kb):
        return slice(0, (kb + 1) * blk) if part == 0 else slice(kb * blk, ev)

    def back(part, h, keep):
        values = halo.at[1] if part == 0 else v_ref
        for kb in range(2):
            rows = slice(kb * blk, (kb + 1) * blk)
            cols = queries(part, kb)
            d_rows = da[cols, head(h)]
            d_w = dot(values[rows, head(h)], d_rows, 1, 1)
            d_s = (d_w * g_s[h, part, rows, cols].astype(F32)).astype(BF)
            g_s[h, part, rows, cols] = d_s
            d_k = dot(d_s, q_ref[cols, head(h)], 1, 0) * scale
            d_v = dot(w_s[h, part, rows, cols], d_rows, 1, 0)
            keep(h, rows, d_k, d_v)

    def keep_far(h, rows, d_k, d_v):
        out_kv[h, 0, rows, :] = d_k.astype(BF)
        out_kv[h, 1, rows, :] = d_v.astype(BF)

    def far(h):
        back(0, h, keep_far)

    def give(h):
        @pl.when(has_left)
        def _():
            grad_copies[h].start()

    def keep_near(h, rows, d_k, d_v):
        att[rows, head(h)] = d_k
        dh[rows, head(h)] = d_v

    def near(h):
        back(1, h, keep_near)

    def query_side(h):
        for b in range(2):
            cols = slice(b * blk, (b + 1) * blk)
            total = 0.0
            for part, keys in ((0, halo.at[0]), (1, k_ref)):
                lo, hi = span(part, b)
                total = total + dot(g_s[h, part, lo:hi, cols], keys[lo:hi, head(h)], 0, 0)
            dq_ref[cols, head(h)] = (total * scale).astype(BF)

    def finish(h):
        @pl.when(has_right)
        def _():
            grad_copies[h].wait_recv()

        dk_ref[:, head(h)] = (att[:, head(h)] + in_kv[h, 0].astype(F32)).astype(BF)
        dv_ref[:, head(h)] = (dh[:, head(h)] + in_kv[h, 1].astype(F32)).astype(BF)

    pending = 0

    def advance():
        nonlocal pending
        if pending < hops - 1:
            for c in range(2):
                land(c, pending)
                launch(c, pending + 1)
            pending += 1

    weight_part()
    launch(0, 0)
    launch(1, 0)
    far(0)
    far(1)
    advance()
    give(0)
    far(2)
    far(3)
    near(0)
    advance()
    give(1)
    near(1)
    near(2)
    near(3)
    advance()
    give(2)
    query_side(0)
    query_side(1)
    advance()
    give(3)
    query_side(2)
    query_side(3)
    while pending < hops - 1:
        advance()
    for h in range(HEADS):
        finish(h)
    root = math.sqrt(total_rows)
    for c in range(2):
        land(c, hops - 1)
        for g in (2 * c, 2 * c + 1):
            dw_ref[:, g * width : (g + 1) * width] = wp[g, 0] / root

    @pl.when(has_right)
    def _():
        for copy in halo_copies:
            copy.wait_send()

    @pl.when(has_left)
    def _():
        for copy in grad_copies:
            copy.wait_send()

    for copies in sum_copies:
        for copy in copies:
            copy.wait_send()


def emit(*refs):
    sems = refs[10]
    copies = [pltpu.make_async_copy(refs[i], refs[5 + i], sems.at[i]) for i in range(5)]
    for copy in copies:
        copy.start()
    for copy in copies:
        copy.wait()


def shards(n, dp, queries, key_rows, value_rows, gate_rows, user_start, w_out, out_grad):
    ev, width = queries.shape[1:]
    model = w_out.shape[1]
    block_rows = width // n
    plans = routes(n, dp)
    hops = len(plans[0])
    legs = [
        pltpu.VMEM((1 if split else 2, size, block_rows, model // 4), BF)
        for plan in plans
        for _, _, size, split in plan
    ]
    rows = pltpu.VMEM((ev, width), BF)
    outs = (rows, rows, rows, rows, pltpu.VMEM((block_rows, model), F32))
    vmem = pl.BlockSpec(memory_space=pltpu.VMEM)
    dma = pltpu.SemaphoreType.DMA
    results = pl.pallas_call(
        functools.partial(kernel, n, dp, dp * n * ev),
        out_shape=outs,
        in_specs=[vmem] + [pl.BlockSpec(memory_space=pl.ANY)] * 6,
        out_specs=(vmem,) * 5,
        scratch_shapes=[
            pltpu.VMEM((ev, width), BF),
            pltpu.VMEM((ev, width), BF),
            pltpu.VMEM((ev, width), BF),
            pltpu.VMEM((ev, width), BF),
            pltpu.VMEM((width, model), BF),
            pltpu.VMEM((ev, model), BF),
            dma((6,)),
            pltpu.VMEM((2, ev, width), BF),
            pltpu.VMEM((HEADS, 2, ev, ev), BF),
            pltpu.VMEM((HEADS, 2, ev, ev), BF),
            pltpu.VMEM((ev, width), F32),
            pltpu.VMEM((ev, width), F32),
            pltpu.VMEM((ev, width), BF),
            pltpu.VMEM((ev, width), BF),
            pltpu.VMEM((HEADS, 2, ev, HS), BF),
            pltpu.VMEM((HEADS, 2, ev, HS), BF),
            pltpu.VMEM((4, n, block_rows, model // 4), F32),
        ]
        + legs
        + legs
        + [dma((2,)), dma((2,)), dma((HEADS,)), dma((HEADS,)), dma((2 * hops,)), dma((2 * hops,))],
        compiler_params=pltpu.CompilerParams(
            collective_id=0, has_side_effects=True, vmem_limit_bytes=60 * 1024 * 1024
        ),
    )(
        user_start, queries[0], key_rows[0], value_rows[0], gate_rows[0], w_out, out_grad[0]
    )
    results = pl.pallas_call(
        emit,
        out_shape=tuple(jax.ShapeDtypeStruct(o.shape, o.dtype) for o in outs),
        in_specs=[vmem] * 5,
        out_specs=(pl.BlockSpec(memory_space=pl.ANY),) * 5,
        scratch_shapes=[dma((5,))],
    )(*[pltpu.with_memory_space_constraint(r, pltpu.VMEM) for r in results])
    return tuple(r[None] for r in results[:4]) + (results[4],)


def solution(mesh):
    n, dp = mesh.shape["hist"], mesh.shape["dp"]
    return jax.shard_map(
        functools.partial(shards, n, dp),
        mesh=mesh,
        in_specs=(
            P("dp", "hist", None),
            P("dp", "hist", None),
            P("dp", "hist", None),
            P("dp", "hist", None),
            P("dp", "hist"),
            P(),
            P("dp", "hist", None),
        ),
        out_specs=(
            P("dp", "hist", None),
            P("dp", "hist", None),
            P("dp", "hist", None),
            P("dp", "hist", None),
            P("hist", None),
        ),
        check_vma=False,
    )
```

```python
import functools
import math

import jax
import jax.numpy as jnp
from jax import lax
from jax.experimental import pallas as pl
from jax.experimental.pallas import tpu as pltpu
from jax.sharding import PartitionSpec as P

HEADS = 4
HS = 128
WIN = 512
EPSILON = 1e-05
BF = jnp.bfloat16
F32 = jnp.float32


def dot(a, b, ca, cb):
    return lax.dot_general(a, b, (((ca,), (cb,)), ((), ())), preferred_element_type=F32)


def routes(n, dp):
    steps, dsteps = n.bit_length() - 1, dp.bit_length() - 1
    plans = []
    for at in (1, 2):
        plan, split = [], False
        for s in range(steps):
            if s == at:
                plan.append(("split", 0, n >> s, True))
                split = True
            plan.append(("hist", s, n >> (s + 1), split))
        plan += [("both", s, 1, True) for s in range(1, dsteps)]
        plan.append(("gather", 0, 1, True))
        plans.append(plan)
    return plans


def kernel(
    n, dp, total_rows,
    st_ref, q_hbm, k_hbm, v_hbm, u_hbm, w_hbm, go_hbm,
    dq_ref, dk_ref, dv_ref, du_ref, dw_ref,
    q_ref, k_ref, v_ref, u_ref, w_ref, go_ref, in_sem,
    halo, w_s, g_s, att, dh, da, hid, out_kv, in_kv, wp, *rest,
):
    steps = n.bit_length() - 1
    dsteps = dp.bit_length() - 1
    plans = routes(n, dp)
    hops = len(plans[0])
    count = 2 * hops
    sends = (rest[:hops], rest[hops:count])
    recvs = (rest[count : count + hops], rest[count + hops : 2 * count])
    ks, kr, gs, gr, ws, wr = rest[2 * count :]
    loads = [
        pltpu.make_async_copy(src, dst, in_sem.at[i])
        for i, (src, dst) in enumerate(
            (
                (k_hbm, k_ref),
                (q_hbm, q_ref),
                (v_hbm, v_ref),
                (w_hbm, w_ref),
                (go_hbm, go_ref),
                (u_hbm, u_ref),
            )
        )
    ]
    for load in loads:
        load.start()
    ev = q_ref.shape[0]
    blk = ev // 2
    me = lax.axis_index("hist")
    mine = lax.axis_index("dp")
    has_left = me > 0
    has_right = me < n - 1
    mesh = pl.DeviceIdType.MESH

    def xor(value, bit):
        return value + bit - 2 * bit * ((value // bit) % 2)

    hist_partners = [{"hist": xor(me, 1 << s)} for s in range(steps)]
    dp_partners = [{"dp": xor(mine, 1 << s)} for s in range(dsteps)]
    partners = hist_partners + dp_partners

    barrier = pltpu.get_barrier_semaphore()
    for partner in partners:
        pl.semaphore_signal(barrier, inc=1, device_id=partner, device_id_type=mesh)

    @pl.when(has_right)
    def _():
        pl.semaphore_signal(barrier, inc=1, device_id={"hist": me + 1}, device_id_type=mesh)

    @pl.when(has_left)
    def _():
        pl.semaphore_signal(barrier, inc=1, device_id={"hist": me - 1}, device_id_type=mesh)

    pl.semaphore_wait(barrier, steps + dsteps + has_left.astype(jnp.int32) + has_right.astype(jnp.int32))

    halo_copies = [
        pltpu.make_async_remote_copy(
            src_ref=ref, dst_ref=halo.at[i], send_sem=ks.at[i], recv_sem=kr.at[i],
            device_id={"hist": me + 1}, device_id_type=mesh,
        )
        for i, ref in enumerate((k_hbm, v_hbm))
    ]
    grad_copies = [
        pltpu.make_async_remote_copy(
            src_ref=out_kv.at[h], dst_ref=in_kv.at[h], send_sem=gs.at[h], recv_sem=gr.at[h],
            device_id={"hist": me - 1}, device_id_type=mesh,
        )
        for h in range(HEADS)
    ]
    sum_copies = [
        [
            pltpu.make_async_remote_copy(
                src_ref=sends[c][i], dst_ref=recvs[c][i],
                send_sem=ws.at[c * hops + i], recv_sem=wr.at[c * hops + i],
                device_id=(hist_partners if kind == "hist" else dp_partners)[s],
                device_id_type=mesh,
            )
            for i, (kind, s, _, _) in enumerate(plans[c])
        ]
        for c in range(2)
    ]

    @pl.when(has_right)
    def _():
        for copy in halo_copies:
            copy.start()

    @pl.when(me == 0)
    def _():
        halo[...] = jnp.zeros_like(halo)

    @pl.when(me == n - 1)
    def _():
        in_kv[...] = jnp.zeros_like(in_kv)

    scale = HS ** (-0.5)
    base = me * ev

    def head(h):
        return slice(h * HS, (h + 1) * HS)

    def mask(part, b, lo, hi):
        cols = slice(b * blk, (b + 1) * blk)
        start = st_ref[:, cols] - base
        jj = lax.broadcasted_iota(jnp.int32, (hi - lo, blk), 0) + lo
        ii = lax.broadcasted_iota(jnp.int32, (hi - lo, blk), 1) + b * blk
        if part == 0:
            live = (jj >= start + ev) & (jj > ii)
        else:
            live = (jj >= start) & (jj <= ii)
        return jnp.where(live, 1.0 / WIN, 0.0).astype(F32)

    def span(part, b):
        return (b * blk, ev) if part == 0 else (0, (b + 1) * blk)

    def scores(part, b, h, keys, live):
        lo, hi = span(part, b)
        cols = slice(b * blk, (b + 1) * blk)
        x = dot(keys[lo:hi, head(h)], q_ref[cols, head(h)], 1, 1) * scale
        sig = 0.5 * jnp.tanh(0.5 * x) + 0.5
        part_sig = sig * live
        wt = x * part_sig
        g_s[h, part, lo:hi, cols] = (part_sig + wt * (1.0 - sig)).astype(BF)
        w_s[h, part, lo:hi, cols] = wt.astype(BF)

    def mix(part, b, h, values):
        lo, hi = span(part, b)
        cols = slice(b * blk, (b + 1) * blk)
        return dot(w_s[h, part, lo:hi, cols], values[lo:hi, head(h)], 0, 0)

    for load in loads[:3]:
        load.wait()
    for b in range(2):
        live = mask(1, b, *span(1, b))
        for h in range(HEADS):
            scores(1, b, h, k_ref, live)
            att[b * blk : (b + 1) * blk, head(h)] = mix(1, b, h, v_ref)
    for load in loads[3:]:
        load.wait()
    for b in range(2):
        rows = slice(b * blk, (b + 1) * blk)
        dh[rows, :] = dot(go_ref[rows, :], w_ref[...], 1, 1)

    @pl.when(has_left)
    def _():
        halo_copies[0].wait_recv()

    for b in range(2):
        live = mask(0, b, *span(0, b))
        for h in range(HEADS):
            scores(0, b, h, halo.at[0], live)

    @pl.when(has_left)
    def _():
        halo_copies[1].wait_recv()

    for b in range(2):
        for h in range(HEADS):
            att[b * blk : (b + 1) * blk, head(h)] += mix(0, b, h, halo.at[1])

    chunk = 256
    @pl.loop(0, ev // chunk)
    def _(c):
        rows = pl.ds(pl.multiple_of(c * chunk, chunk), chunk)
        a = att[rows, :]
        centred = a - jnp.mean(a, axis=-1, keepdims=True)
        inverse = lax.rsqrt(jnp.mean(centred * centred, axis=-1, keepdims=True) + EPSILON)
        normed = centred * inverse
        gate = u_ref[rows, :].astype(F32)
        hid[rows, :] = (normed * gate).astype(BF)
        d_hidden = dh[rows, :]
        du_ref[rows, :] = (d_hidden * normed).astype(BF)
        d_normed = d_hidden * gate
        d_attn = inverse * (
            d_normed
            - jnp.mean(d_normed, axis=-1, keepdims=True)
            - normed * jnp.mean(d_normed * normed, axis=-1, keepdims=True)
        )
        da[rows, :] = d_attn.astype(BF)

    block_rows = wp.shape[2]
    width = wp.shape[3]
    low = mine % 2

    def weight_part():
        whole = dot(hid[...], go_ref[...], 0, 0)
        for g in range(4):
            wp[g] = whole[:, g * width : (g + 1) * width].reshape(n, block_rows, width)

    def groups(c, split):
        return [2 * c + low] if split else [2 * c, 2 * c + 1]

    def launch(c, i):
        kind, s, size, split = plans[c][i]
        target = sends[c][i]
        if kind == "hist":
            bit = (me // (1 << s)) % 2
            for a, g in enumerate(groups(c, split)):
                for j in range(size):
                    target[a, j] = wp[g, 2 * j + 1 - bit].astype(BF)
        elif kind == "split":
            for j in range(size):
                target[0, j] = wp[2 * c + 1 - low, j].astype(BF)
        else:
            target[0, 0] = wp[2 * c + low, 0].astype(BF)
        sum_copies[c][i].start()

    def land(c, i):
        kind, s, size, split = plans[c][i]
        source = recvs[c][i]
        sum_copies[c][i].wait_recv()
        if kind == "hist":
            bit = (me // (1 << s)) % 2
            for a, g in enumerate(groups(c, split)):
                for j in range(size):
                    wp[g, j] = wp[g, 2 * j + bit] + source[a, j].astype(F32)
        elif kind == "split":
            for j in range(size):
                wp[2 * c + low, j] = wp[2 * c + low, j] + source[0, j].astype(F32)
        elif kind == "both":
            wp[2 * c + low, 0] = sends[c][i][0, 0].astype(F32) + source[0, 0].astype(F32)
        else:
            wp[2 * c + low, 0] = sends[c][i][0, 0].astype(F32)
            wp[2 * c + 1 - low, 0] = source[0, 0].astype(F32)

    def queries(part, kb):
        return slice(0, (kb + 1) * blk) if part == 0 else slice(kb * blk, ev)

    def back(part, h, keep):
        values = halo.at[1] if part == 0 else v_ref
        for kb in range(2):
            rows = slice(kb * blk, (kb + 1) * blk)
            cols = queries(part, kb)
            d_rows = da[cols, head(h)]
            d_w = dot(values[rows, head(h)], d_rows, 1, 1)
            d_s = (d_w * g_s[h, part, rows, cols].astype(F32)).astype(BF)
            g_s[h, part, rows, cols] = d_s
            d_k = dot(d_s, q_ref[cols, head(h)], 1, 0) * scale
            d_v = dot(w_s[h, part, rows, cols], d_rows, 1, 0)
            keep(h, rows, d_k, d_v)

    def keep_far(h, rows, d_k, d_v):
        out_kv[h, 0, rows, :] = d_k.astype(BF)
        out_kv[h, 1, rows, :] = d_v.astype(BF)

    def far(h):
        back(0, h, keep_far)

    def give(h):
        @pl.when(has_left)
        def _():
            grad_copies[h].start()

    def keep_near(h, rows, d_k, d_v):
        att[rows, head(h)] = d_k
        dh[rows, head(h)] = d_v

    def near(h):
        back(1, h, keep_near)

    def query_side(h):
        for b in range(2):
            cols = slice(b * blk, (b + 1) * blk)
            total = 0.0
            for part, keys in ((0, halo.at[0]), (1, k_ref)):
                lo, hi = span(part, b)
                total = total + dot(g_s[h, part, lo:hi, cols], keys[lo:hi, head(h)], 0, 0)
            dq_ref[cols, head(h)] = (total * scale).astype(BF)

    def finish(h):
        @pl.when(has_right)
        def _():
            grad_copies[h].wait_recv()

        dk_ref[:, head(h)] = (att[:, head(h)] + in_kv[h, 0].astype(F32)).astype(BF)
        dv_ref[:, head(h)] = (dh[:, head(h)] + in_kv[h, 1].astype(F32)).astype(BF)

    pending = 0

    def advance():
        nonlocal pending
        if pending < hops - 1:
            for c in range(2):
                land(c, pending)
                launch(c, pending + 1)
            pending += 1

    weight_part()
    launch(0, 0)
    launch(1, 0)
    far(0)
    advance()
    far(1)
    far(2)
    far(3)
    advance()
    give(0)
    near(0)
    near(1)
    near(2)
    advance()
    give(1)
    near(3)
    query_side(0)
    advance()
    give(2)
    give(3)
    query_side(1)
    query_side(2)
    query_side(3)
    while pending < hops - 1:
        advance()
    for h in range(HEADS):
        finish(h)
    root = math.sqrt(total_rows)
    for c in range(2):
        land(c, hops - 1)
        for g in (2 * c, 2 * c + 1):
            dw_ref[:, g * width : (g + 1) * width] = wp[g, 0] / root

    @pl.when(has_right)
    def _():
        for copy in halo_copies:
            copy.wait_send()

    @pl.when(has_left)
    def _():
        for copy in grad_copies:
            copy.wait_send()

    for copies in sum_copies:
        for copy in copies:
            copy.wait_send()


def emit(*refs):
    sems = refs[10]
    copies = [pltpu.make_async_copy(refs[i], refs[5 + i], sems.at[i]) for i in range(5)]
    for copy in copies:
        copy.start()
    for copy in copies:
        copy.wait()


def shards(n, dp, queries, key_rows, value_rows, gate_rows, user_start, w_out, out_grad):
    ev, width = queries.shape[1:]
    model = w_out.shape[1]
    block_rows = width // n
    plans = routes(n, dp)
    hops = len(plans[0])
    legs = [
        pltpu.VMEM((1 if split else 2, size, block_rows, model // 4), BF)
        for plan in plans
        for _, _, size, split in plan
    ]
    rows = pltpu.VMEM((ev, width), BF)
    outs = (rows, rows, rows, rows, pltpu.VMEM((block_rows, model), F32))
    vmem = pl.BlockSpec(memory_space=pltpu.VMEM)
    dma = pltpu.SemaphoreType.DMA
    results = pl.pallas_call(
        functools.partial(kernel, n, dp, dp * n * ev),
        out_shape=outs,
        in_specs=[vmem] + [pl.BlockSpec(memory_space=pl.ANY)] * 6,
        out_specs=(vmem,) * 5,
        scratch_shapes=[
            pltpu.VMEM((ev, width), BF),
            pltpu.VMEM((ev, width), BF),
            pltpu.VMEM((ev, width), BF),
            pltpu.VMEM((ev, width), BF),
            pltpu.VMEM((width, model), BF),
            pltpu.VMEM((ev, model), BF),
            dma((6,)),
            pltpu.VMEM((2, ev, width), BF),
            pltpu.VMEM((HEADS, 2, ev, ev), BF),
            pltpu.VMEM((HEADS, 2, ev, ev), BF),
            pltpu.VMEM((ev, width), F32),
            pltpu.VMEM((ev, width), F32),
            pltpu.VMEM((ev, width), BF),
            pltpu.VMEM((ev, width), BF),
            pltpu.VMEM((HEADS, 2, ev, HS), BF),
            pltpu.VMEM((HEADS, 2, ev, HS), BF),
            pltpu.VMEM((4, n, block_rows, model // 4), F32),
        ]
        + legs
        + legs
        + [dma((2,)), dma((2,)), dma((HEADS,)), dma((HEADS,)), dma((2 * hops,)), dma((2 * hops,))],
        compiler_params=pltpu.CompilerParams(
            collective_id=0, has_side_effects=True, vmem_limit_bytes=60 * 1024 * 1024
        ),
    )(
        user_start, queries[0], key_rows[0], value_rows[0], gate_rows[0], w_out, out_grad[0]
    )
    results = pl.pallas_call(
        emit,
        out_shape=tuple(jax.ShapeDtypeStruct(o.shape, o.dtype) for o in outs),
        in_specs=[vmem] * 5,
        out_specs=(pl.BlockSpec(memory_space=pl.ANY),) * 5,
        scratch_shapes=[dma((5,))],
    )(*[pltpu.with_memory_space_constraint(r, pltpu.VMEM) for r in results])
    return tuple(r[None] for r in results[:4]) + (results[4],)


def solution(mesh):
    n, dp = mesh.shape["hist"], mesh.shape["dp"]
    return jax.shard_map(
        functools.partial(shards, n, dp),
        mesh=mesh,
        in_specs=(
            P("dp", "hist", None),
            P("dp", "hist", None),
            P("dp", "hist", None),
            P("dp", "hist", None),
            P("dp", "hist"),
            P(),
            P("dp", "hist", None),
        ),
        out_specs=(
            P("dp", "hist", None),
            P("dp", "hist", None),
            P("dp", "hist", None),
            P("dp", "hist", None),
            P("hist", None),
        ),
        check_vma=False,
    )
```
